32 devices in a mesh: grp: 2 (over y), tile: 4 (over z), sub: 4 (over x, core).
Axes of the slice: x: 2, y: 2, z: 4, core: 2. Of those that a mesh axis runs over, the one named last changes fastest.
Arguments:
- features: bfloat16 [24, 32, 1024], P(('grp', 'tile'), 'sub'), parts along dimension 0, may hold values from -6 to 6
- out_grad: bfloat16 [24, 32, 1024], P(('grp', 'tile'), 'sub'), parts along dimension 0, may hold values from -6 to 6
- filters: bfloat16 [5, 32, 32], replicated, may hold values from -0.5 to 0.5
- tile_map: int32 [12], replicated, may hold values from 0 to 11, as said below
Outputs:
- in_grad: bfloat16 [24, 32, 1024], P(('grp', 'tile'), 'sub'), parts along dimension 0
- weight_grad: float32 [10, 32, 32], P('grp', 'sub'), parts along dimension 0
The draws below stay inside these ranges and needn't reach their ends.
There are 2 independent parts, one for each index of `grp`. The reference program is written for one: setup_inputs(seed, part) draws one part's arguments, and reference() takes and returns one part's arrays. A program takes and returns all parts, laid end to end along the dimension named above; an argument that names none is the same for every part. Nothing has to cross between parts.
Inputs may be any that keep to these rules, and one draw needn't show every extreme that they name: tile_map[s] is the nested index of the tile held in slot s; slots 3 * j to 3 * j + 2 lie on index j of tile and hold the nested indices 3 * j to 3 * j + 2 in some order.
All inputs are finite; a program needn't handle non-finite values.
Results may differ from the reference program's by a relative error of at most 0.00045.
Values may be sent and summed in bfloat16 or wider, within the bound.
No kernel may reach another device: no remote copies, remote signals or barrier semaphores. Data moves between devices by JAX's collectives and lax.ppermute only.
A program may use at most 64 MiB of HBM per device.

```python
import math
import jax
import jax.numpy as jnp
from jax import lax

C = 32
K = 5
TPD = 3
TS = 32
Q = 1
TILES = 12
PIXELS = 12288


def draw_tile_map(key, part):
    blocks = jnp.arange(TILES, dtype=jnp.int32).reshape(TILES // TPD, TPD)
    shuffled = jax.random.permutation(key, blocks, axis=1, independent=True)
    return shuffled.reshape(TILES).astype(jnp.int32)


def shard_levels(stream_key, shape, pieces, smallest, largest):
    def one(dim, blocks):
        draws = jax.random.uniform(jax.random.fold_in(jax.random.fold_in(stream_key, 6), dim), (blocks,), jnp.float32, smallest / len(pieces), largest / len(pieces))
        return jnp.repeat(jnp.exp(draws), shape[dim] // blocks).reshape((-1,) + (1,) * (len(shape) - dim - 1))

    factor_of = one(*pieces[0])
    for cut in pieces[1:]:
        factor_of = factor_of * one(*cut)
    return factor_of


def noise(own_key, shape, spread, limit, cuts=(), kind=jnp.bfloat16):
    result = jax.random.normal(own_key, shape, jnp.float32) * spread
    if len(cuts) > 0:
        result = shard_levels(own_key, shape, cuts, -0.22, 0.18) * result
    return jnp.clip(result, min=-limit, max=limit).astype(kind)


def setup_inputs(seed: int = 0, part: int = 0) -> dict:
    streams_of = jax.random.split(jax.random.key(seed), 5)
    own_keys = jax.random.split(jax.random.fold_in(streams_of[4], part), 5)
    features = noise(own_keys[0], (TILES, C, TS * TS), 1.0, 6.0, ((0, 4), (1, 4)))
    out_grad = noise(own_keys[1], (TILES, C, TS * TS), 1.0, 6.0, ((0, 4), (1, 4)))
    filters = noise(streams_of[2], (K, C, C), (K * C) ** -0.5, 0.5)
    tile_map = draw_tile_map(jax.random.fold_in(streams_of[4], 71), part)
    return dict(features=features, out_grad=out_grad, filters=filters, tile_map=tile_map)


def tile_coords(nested_code, bit_count):
    coord_x = nested_code * 0
    coord_y = nested_code * 0
    for bit_level in range(bit_count):
        coord_x = coord_x + nested_code // 4 ** bit_level % 2 * 2 ** bit_level
        coord_y = coord_y + nested_code // (2 * 4 ** bit_level) % 2 * 2 ** bit_level
    return (coord_x, coord_y)

def nested_index(coord_x, coord_y, bit_count):
    nested_code = coord_x * 0
    for bit_level in range(bit_count):
        nested_code = nested_code + coord_x // 2 ** bit_level % 2 * 4 ** bit_level
        nested_code = nested_code + coord_y // 2 ** bit_level % 2 * (2 * 4 ** bit_level)
    return nested_code

def pick(condition, when_true, when_false):
    return when_false + (when_true - when_false) * condition

def neighbour_codes(tile_ids, per_face, side_count):
    bit_count = side_count.bit_length() - 1
    face_id = tile_ids // per_face
    coord_x, coord_y = tile_coords(tile_ids % per_face, bit_count)
    column = face_id % 4
    is_north = face_id < 4
    is_south = face_id >= 8
    last_tile = side_count - 1

    def by_cycle(north_value, equator_value, south_value):
        return pick(is_north, north_value, pick(is_south, south_value, equator_value))
    side_rules = [(coord_x > 0, (face_id, coord_x - 1, coord_y, 1), (by_cycle(4 + column, 8 + (column + 3) % 4, 8 + (column + 3) % 4), by_cycle(last_tile, last_tile, coord_y), by_cycle(coord_y, coord_y, 0), by_cycle(1, 1, 2))), (coord_x < last_tile, (face_id, coord_x + 1, coord_y, 0), (by_cycle((column + 1) % 4, column, 4 + (column + 1) % 4), by_cycle(coord_y, 0, 0), by_cycle(last_tile, coord_y, coord_y), by_cycle(3, 0, 0))), (coord_y > 0, (face_id, coord_x, coord_y - 1, 3), (by_cycle(4 + (column + 1) % 4, 8 + column, 8 + (column + 1) % 4), by_cycle(coord_x, coord_x, 0), by_cycle(last_tile, last_tile, coord_x), by_cycle(3, 3, 0))), (coord_y < last_tile, (face_id, coord_x, coord_y + 1, 2), (by_cycle((column + 3) % 4, (column + 3) % 4, 4 + column), by_cycle(last_tile, coord_x, coord_x), by_cycle(coord_x, 0, 0), by_cycle(1, 2, 2)))]
    target_list = []
    edge_list = []
    for inside, within, across in side_rules:
        chosen = [pick(inside, near_value, far_value) for near_value, far_value in zip(within, across)]
        target_list.append(chosen[0] * per_face + nested_index(chosen[1], chosen[2], bit_count))
        edge_list.append(chosen[3] + tile_ids * 0)
    return (target_list, edge_list)

def neighbour_table(tile_map, per_face, side_count):
    target_list, edge_list = neighbour_codes(tile_map, per_face, side_count)
    targets = jnp.stack(target_list, axis=1).astype(jnp.int32)
    edges = jnp.stack(edge_list, axis=1).astype(jnp.int32)
    slot_of = jnp.argsort(tile_map).astype(jnp.int32)
    return (slot_of[targets].astype(jnp.int32), edges)

def edge_lines(values, tile_side):
    return jnp.stack([values[..., :tile_side], values[..., -tile_side:], values[..., ::tile_side], values[..., tile_side - 1::tile_side]], axis=1)

def stencil(values, ghosts, tile_side):
    position = jnp.arange(values.shape[-1]) % tile_side
    zero_line = jnp.zeros_like(values[..., :1])
    upper_side = jnp.concatenate([ghosts[:, 0], values[..., :-tile_side]], axis=-1)
    lower_side = jnp.concatenate([values[..., tile_side:], ghosts[:, 1]], axis=-1)
    left_side = jnp.where(position == 0, jnp.repeat(ghosts[:, 2], tile_side, axis=-1), jnp.concatenate([zero_line, values[..., :-1]], axis=-1))
    right_side = jnp.where(position == tile_side - 1, jnp.repeat(ghosts[:, 3], tile_side, axis=-1), jnp.concatenate([values[..., 1:], zero_line], axis=-1))
    return -0.25 * (upper_side + lower_side + left_side + right_side)

def reference(features, out_grad, filters, tile_map):
    slot_table, edge_table = neighbour_table(tile_map, TILES // 12, Q)
    highest = lax.Precision.HIGHEST

    def laplace(values):
        return stencil(values, edge_lines(values, TS)[slot_table, edge_table], TS)
    inputs = features.astype(jnp.float32)
    cotangent = out_grad.astype(jnp.float32)
    weights = filters.astype(jnp.float32)
    previous, current = (inputs, laplace(inputs))
    filter_terms = [jnp.einsum('sip,sop->io', inputs, cotangent, precision=highest), jnp.einsum('sip,sop->io', current, cotangent, precision=highest)]
    for degree in range(2, K):
        previous, current = (current, 2.0 * laplace(current) - previous)
        filter_terms.append(jnp.einsum('sip,sop->io', current, cotangent, precision=highest))
    weight_grad = jnp.stack(filter_terms) / math.sqrt(PIXELS)

    def mixed(degree):
        return jnp.einsum('sop,io->sip', cotangent, weights[degree], precision=highest)
    next_sum = mixed(K - 1)
    after_next = jnp.zeros_like(next_sum)
    for degree in range(K - 2, 0, -1):
        next_sum, after_next = (mixed(degree) + 2.0 * laplace(next_sum) - after_next, next_sum)
    in_grad = (mixed(0) + laplace(next_sum) - after_next).astype(jnp.bfloat16)
    return (in_grad, weight_grad)
```

```python
import functools
import math

import jax
import jax.numpy as jnp
import numpy as np
from jax import lax
from jax.experimental import pallas as pl
from jax.experimental.pallas import tpu as pltpu
from jax.sharding import PartitionSpec as P

K = 5


def from_behind(value, axis, steps):
    count = lax.axis_size(axis)
    pairs = [(source, (source + steps) % count) for source in range(count)]
    return lax.ppermute(value, axis, pairs)


def tile_coords(nested_code, bit_count):
    coord_x = nested_code * 0
    coord_y = nested_code * 0
    for bit_level in range(bit_count):
        coord_x = coord_x + nested_code // 4**bit_level % 2 * 2**bit_level
        coord_y = coord_y + nested_code // (2 * 4**bit_level) % 2 * 2**bit_level
    return (coord_x, coord_y)


def nested_index(coord_x, coord_y, bit_count):
    nested_code = coord_x * 0
    for bit_level in range(bit_count):
        nested_code = nested_code + coord_x // 2**bit_level % 2 * 4**bit_level
        nested_code = nested_code + coord_y // 2**bit_level % 2 * (2 * 4**bit_level)
    return nested_code


def pick(condition, when_true, when_false):
    return when_false + (when_true - when_false) * condition


def neighbour_codes(tile_ids, per_face, side_count):
    bit_count = side_count.bit_length() - 1
    face_id = tile_ids // per_face
    coord_x, coord_y = tile_coords(tile_ids % per_face, bit_count)
    column = face_id % 4
    is_north = face_id < 4
    is_south = face_id >= 8
    last_tile = side_count - 1

    def by_cycle(north_value, equator_value, south_value):
        return pick(is_north, north_value, pick(is_south, south_value, equator_value))

    side_rules = [
        (
            coord_x > 0,
            (face_id, coord_x - 1, coord_y, 1),
            (
                by_cycle(4 + column, 8 + (column + 3) % 4, 8 + (column + 3) % 4),
                by_cycle(last_tile, last_tile, coord_y),
                by_cycle(coord_y, coord_y, 0),
                by_cycle(1, 1, 2),
            ),
        ),
        (
            coord_x < last_tile,
            (face_id, coord_x + 1, coord_y, 0),
            (
                by_cycle((column + 1) % 4, column, 4 + (column + 1) % 4),
                by_cycle(coord_y, 0, 0),
                by_cycle(last_tile, coord_y, coord_y),
                by_cycle(3, 0, 0),
            ),
        ),
        (
            coord_y > 0,
            (face_id, coord_x, coord_y - 1, 3),
            (
                by_cycle(4 + (column + 1) % 4, 8 + column, 8 + (column + 1) % 4),
                by_cycle(coord_x, coord_x, 0),
                by_cycle(last_tile, last_tile, coord_x),
                by_cycle(3, 3, 0),
            ),
        ),
        (
            coord_y < last_tile,
            (face_id, coord_x, coord_y + 1, 2),
            (
                by_cycle((column + 3) % 4, (column + 3) % 4, 4 + column),
                by_cycle(last_tile, coord_x, coord_x),
                by_cycle(coord_x, 0, 0),
                by_cycle(1, 2, 2),
            ),
        ),
    ]
    target_list = []
    edge_list = []
    for inside, within, across in side_rules:
        chosen = [
            pick(inside, near_value, far_value) for near_value, far_value in zip(within, across)
        ]
        target_list.append(chosen[0] * per_face + nested_index(chosen[1], chosen[2], bit_count))
        edge_list.append(chosen[3] + tile_ids * 0)
    return (target_list, edge_list)


def neighbour_table(tile_map, per_face, side_count):
    target_list, edge_list = neighbour_codes(tile_map, per_face, side_count)
    targets = jnp.stack(target_list, axis=1).astype(jnp.int32)
    edges = jnp.stack(edge_list, axis=1).astype(jnp.int32)
    slot_of = jnp.argsort(tile_map).astype(jnp.int32)
    return (slot_of[targets].astype(jnp.int32), edges)


def peer_offsets(slot_count, device_count, per_face, side_count):
    tile_ids = np.arange(slot_count * device_count, dtype=np.int64)
    target_list, edge_list = neighbour_codes(tile_ids, per_face, side_count)
    targets = np.stack(target_list, axis=1)
    offsets = (tile_ids[:, None] // slot_count - targets // slot_count) % device_count
    distinct = sorted(set((int(value) for value in offsets.ravel())) - {0})
    position = np.zeros(device_count, dtype=np.int32)
    for order, value in enumerate(distinct):
        position[value] = order + 1
    return (distinct, position)


def edge_lines(values, tile_side):
    return jnp.stack(
        [
            values[..., :tile_side],
            values[..., -tile_side:],
            values[..., ::tile_side],
            values[..., tile_side - 1 :: tile_side],
        ],
        axis=1,
    )


def stencil(values, ghosts, tile_side):
    position = jnp.arange(values.shape[-1]) % tile_side
    zero_line = jnp.zeros_like(values[..., :1])
    upper_side = jnp.concatenate([ghosts[:, 0], values[..., :-tile_side]], axis=-1)
    lower_side = jnp.concatenate([values[..., tile_side:], ghosts[:, 1]], axis=-1)
    left_side = jnp.where(
        position == 0,
        jnp.repeat(ghosts[:, 2], tile_side, axis=-1),
        jnp.concatenate([zero_line, values[..., :-1]], axis=-1),
    )
    right_side = jnp.where(
        position == tile_side - 1,
        jnp.repeat(ghosts[:, 3], tile_side, axis=-1),
        jnp.concatenate([values[..., 1:], zero_line], axis=-1),
    )
    return -0.25 * (upper_side + lower_side + left_side + right_side)


def tile_total(filter_part):
    return lax.psum(filter_part, "tile")


def by_halos(features, out_grad, filters, tile_map):
    slot_count = features.shape[0]
    group_channels = features.shape[1]
    tile_side = math.isqrt(features.shape[2])
    device_count = lax.axis_size("tile")
    total_tiles = slot_count * device_count
    side_count = math.isqrt(total_tiles // 12)
    scale_factor = 1.0 / math.sqrt(total_tiles * features.shape[2])
    highest = lax.Precision.HIGHEST
    slot_table, edge_table = neighbour_table(tile_map, total_tiles // 12, side_count)
    my_device = lax.axis_index("tile")
    first_slot = my_device * slot_count
    my_slots = lax.dynamic_slice_in_dim(slot_table, first_slot, slot_count, 0)
    my_edges = lax.dynamic_slice_in_dim(edge_table, first_slot, slot_count, 0)
    channel_start = lax.axis_index("sub") * group_channels
    weights = filters.astype(jnp.float32)
    distinct, position = peer_offsets(slot_count, device_count, total_tiles // 12, side_count)
    sender_gap = (my_device - my_slots // slot_count) % device_count
    local_rows = jnp.asarray(position)[sender_gap] * slot_count + my_slots % slot_count

    def laplace(values):
        border = edge_lines(values, tile_side).reshape(slot_count, 4, group_channels * tile_side)
        received = [border]
        for offset_value in distinct:
            received.append(from_behind(border, "tile", offset_value))
        stacked = jnp.concatenate(received, axis=0)
        stacked = stacked.reshape(stacked.shape[0], 4, group_channels, tile_side)
        ghosts = stacked[local_rows, my_edges]
        return stencil(values, ghosts, tile_side)

    whole_grad = lax.all_gather(out_grad, "sub", axis=1, tiled=True)
    cotangent = whole_grad.astype(jnp.float32)
    inputs = features.astype(jnp.float32)
    previous, current = (inputs, laplace(inputs))
    filter_terms = [
        jnp.einsum("sip,sop->io", inputs, cotangent, precision=highest),
        jnp.einsum("sip,sop->io", current, cotangent, precision=highest),
    ]
    for degree in range(2, K):
        previous, current = (current, 2.0 * laplace(current) - previous)
        filter_terms.append(jnp.einsum("sip,sop->io", current, cotangent, precision=highest))
    weight_grad = tile_total(jnp.stack(filter_terms)) * scale_factor
    row_block = lax.dynamic_slice_in_dim(weights, channel_start, group_channels, 1)

    def mixed(degree):
        return jnp.einsum("sop,io->sip", cotangent, row_block[degree], precision=highest)

    next_sum = mixed(K - 1)
    after_next = jnp.zeros_like(next_sum)
    for degree in range(K - 2, 0, -1):
        next_sum, after_next = (mixed(degree) + 2.0 * laplace(next_sum) - after_next, next_sum)
    in_grad = (mixed(0) + laplace(next_sum) - after_next).astype(jnp.bfloat16)
    return (in_grad, weight_grad)


LANES = 128
GATHER_LIMIT = 2 << 20


def lane_gather(block, lane_index):
    index = jnp.broadcast_to(lane_index, block.shape)
    return jnp.take_along_axis(block, index, axis=1, mode="promise_in_bounds")


class FaceStencil:
    def __init__(self, tile_count, tile_side):
        per_face = tile_count // 12
        side_count = math.isqrt(per_face)
        targets, edges = neighbour_codes(
            np.arange(tile_count, dtype=np.int64), per_face, side_count
        )
        self.targets = np.stack(targets, axis=1)
        self.edges = np.stack(edges, axis=1)
        self.side = tile_side
        self.rows = LANES // tile_side
        self.blocks = tile_side * tile_side // LANES
        self.lane = lax.broadcasted_iota(jnp.int32, (1, LANES), 1)

    def block(self, ref, tile, number):
        return ref[tile, :, number * LANES : (number + 1) * LANES]

    def row_as_row(self, ref, tile, edge):
        if edge == 0:
            return self.block(ref, tile, 0)
        return self.block(ref, tile, self.blocks - 1)

    def column_as_row(self, ref, tile, edge, first_lane):
        lane, side, rows = self.lane, self.side, self.rows
        column = 0 if edge == 2 else side - 1
        place = lane - first_lane
        index = place % rows * side + column
        index = jnp.where((place >= 0) & (place < side), index, 0)
        line = lane_gather(self.block(ref, tile, 0), index)
        for number in range(1, self.blocks):
            moved = lane_gather(self.block(ref, tile, number), index)
            line = jnp.where(place // rows == number, moved, line)
        return line

    def row_as_column(self, ref, tile, edge):
        block = self.row_as_row(ref, tile, edge)
        base = 0 if edge == 0 else LANES - self.side
        return [
            lane_gather(block, self.lane // self.side + (base + number * self.rows))
            for number in range(self.blocks)
        ]

    def neighbour_sum(self, ref, tile):
        lane, side, last = self.lane, self.side, self.blocks - 1
        target, edge = self.targets[tile], self.edges[tile]
        value = [self.block(ref, tile, number) for number in range(self.blocks)]

        if edge[0] == 1:
            above = self.row_as_row(ref, target[0], 1)
        elif edge[0] == 0:
            above = pltpu.roll(self.row_as_row(ref, target[0], 0), LANES - side, 1)
        else:
            above = self.column_as_row(ref, target[0], edge[0], LANES - side)
        down_turn = [pltpu.roll(block, side, 1) for block in [above] + value]
        upper = [
            jnp.where(lane < side, down_turn[number], down_turn[number + 1])
            for number in range(self.blocks)
        ]
        if edge[1] == 0:
            below = self.row_as_row(ref, target[1], 0)
        elif edge[1] == 1:
            below = pltpu.roll(self.row_as_row(ref, target[1], 1), side, 1)
        else:
            below = self.column_as_row(ref, target[1], edge[1], 0)
        up_turn = [pltpu.roll(block, LANES - side, 1) for block in value + [below]]
        lower = [
            jnp.where(lane >= LANES - side, up_turn[number + 1], up_turn[number])
            for number in range(self.blocks)
        ]
        column = lane % side
        row_start = lane - column
        if edge[2] >= 2:
            beside = [self.block(ref, target[2], number) for number in range(self.blocks)]
            if edge[2] == 2:
                turn = row_start + (column + 1) % side
                beside = [lane_gather(block, turn) for block in beside]
        else:
            beside = self.row_as_column(ref, target[2], edge[2])
        turn = row_start + (column + side - 1) % side
        left = [
            lane_gather(jnp.where(column == side - 1, ghost, block), turn)
            for ghost, block in zip(beside, value)
        ]
        if edge[3] >= 2:
            beside = [self.block(ref, target[3], number) for number in range(self.blocks)]
            if edge[3] == 3:
                turn = row_start + (column + side - 1) % side
                beside = [lane_gather(block, turn) for block in beside]
        else:
            beside = self.row_as_column(ref, target[3], edge[3])
        turn = row_start + (column + 1) % side
        right = [
            lane_gather(jnp.where(column == 0, ghost, block), turn)
            for ghost, block in zip(beside, value)
        ]
        return [
            (upper[number] + lower[number]) + (left[number] + right[number])
            for number in range(self.blocks)
        ]


def split_rows(value):
    high = value.astype(jnp.bfloat16).astype(jnp.float32)
    return jnp.concatenate([high, value - high], axis=0).astype(jnp.bfloat16)


def features_kernel(pieces, slot_count, tile_count, tile_side, map_ref, *refs):
    piece_refs, out_ref, terms = refs[:pieces], refs[pieces], refs[pieces + 1]
    grid = FaceStencil(tile_count, tile_side)
    me = lax.axis_index("tile")
    for piece in range(pieces):
        for slot in range(slot_count):
            place = map_ref[(me ^ piece) * slot_count + slot]
            terms[0, place] = piece_refs[piece][slot].astype(jnp.float32)
    for tile in range(tile_count):
        out_ref[tile, 0:16] = split_rows(terms[0, tile])
    for degree in range(1, K):
        source = terms.at[degree - 1]
        for tile in range(tile_count):
            sums = grid.neighbour_sum(source, tile)
            for number, total in enumerate(sums):
                lanes = slice(number * LANES, (number + 1) * LANES)
                if degree == 1:
                    term = -0.25 * total
                else:
                    term = -0.5 * total - terms[degree - 2, tile, :, lanes]
                terms[degree, tile, :, lanes] = term
                out_ref[tile, 16 * degree : 16 * degree + 16, lanes] = split_rows(term)


def gradient_kernel(
    pieces, groups, slot_count, tile_count, tile_side, scale_factor, map_ref, *refs
):
    group_refs = refs[:groups]
    terms_ref, filters_ref, in_grad_ref, weight_grad_ref = refs[groups : groups + 4]
    whole, weights, mixed, sums_a, sums_b = refs[groups + 4 :]
    grid = FaceStencil(tile_count, tile_side)
    me = lax.axis_index("tile")
    group = lax.axis_index("sub")
    group_channels = group_refs[0].shape[1]
    channels = groups * group_channels

    for piece in range(pieces):
        for slot in range(slot_count):
            place = map_ref[(me ^ piece) * slot_count + slot]
            rows = [
                group_refs[other][piece * slot_count + slot].astype(jnp.float32)
                for other in range(groups)
            ]
            whole[place] = jnp.concatenate(rows, axis=0).astype(jnp.bfloat16)

    lane = lax.broadcasted_iota(jnp.int32, (1, LANES), 1)
    order = jnp.where(lane < channels, lane ^ (group * group_channels), lane)
    weights[...] = jnp.zeros_like(weights)
    weights[:, :, 0:channels] = filters_ref[...].astype(jnp.float32)
    first = pl.multiple_of(group * group_channels, group_channels)
    rows = [
        lane_gather(weights[degree, pl.ds(first, group_channels), :], order)[:, :channels]
        for degree in range(K)
    ]
    row_block = jnp.concatenate(rows, axis=0).astype(jnp.bfloat16)

    total = jnp.zeros((16 * K, channels), jnp.float32)
    for tile in range(tile_count):
        cotangent = whole[tile]
        mixed[tile] = jnp.dot(row_block, cotangent, preferred_element_type=jnp.float32)
        total = total + lax.dot_general(
            terms_ref[tile],
            cotangent,
            (((1,), (1,)), ((), ())),
            preferred_element_type=jnp.float32,
        )
    total = jnp.concatenate(
        [total, jnp.zeros((16 * K, LANES - channels), jnp.float32)], axis=1
    )
    for degree in range(K):
        high = total[16 * degree : 16 * degree + 8]
        low = total[16 * degree + 8 : 16 * degree + 16]
        part = lane_gather((high + low) * scale_factor, order)
        weight_grad_ref[degree] = part[:, :channels]

    def term(degree, tile, lanes):
        first_row = degree * group_channels
        return mixed[tile, first_row : first_row + group_channels, lanes]

    whole_lanes = slice(0, tile_side * tile_side)
    for tile in range(tile_count):
        sums_a[tile] = term(K - 1, tile, whole_lanes)
    current, other = sums_a, sums_b
    for degree in range(K - 2, -1, -1):
        for tile in range(tile_count):
            sums = grid.neighbour_sum(current, tile)
            for number, neighbours in enumerate(sums):
                lanes = slice(number * LANES, (number + 1) * LANES)
                factor = -0.5 if degree > 0 else -0.25
                value = term(degree, tile, lanes) + factor * neighbours
                if degree < K - 2:
                    value = value - other[tile, :, lanes]
                other[tile, :, lanes] = value
        current, other = other, current
    for slot in range(slot_count):
        place = map_ref[me * slot_count + slot]
        in_grad_ref[slot] = current[place].astype(jnp.bfloat16)


def by_gathering(features, out_grad, filters, tile_map):
    slot_count, group_channels, pixels = features.shape
    tile_side = math.isqrt(pixels)
    device_count = lax.axis_size("tile")
    groups = lax.axis_size("sub")
    tile_count = slot_count * device_count
    scale_factor = 1.0 / math.sqrt(tile_count * pixels)

    def exchanged(value, axis, distance):
        count = lax.axis_size(axis)
        return lax.ppermute(value, axis, [(index, index ^ distance) for index in range(count)])

    order = range(device_count - 1, 0, -1)
    cotangents = {0: out_grad}
    for distance in order:
        cotangents[distance] = exchanged(out_grad, "tile", distance)
    inputs = {0: features}
    for distance in order:
        inputs[distance] = exchanged(features, "tile", distance)
    stacked = jnp.concatenate([cotangents[piece] for piece in range(device_count)], axis=0)
    by_group = {0: stacked}
    distance = groups // 2
    while distance:
        for known in list(by_group):
            by_group[known + distance] = exchanged(by_group[known], "sub", distance)
        distance //= 2

    in_smem = pl.BlockSpec(memory_space=pltpu.SMEM)
    in_vmem = pl.BlockSpec(memory_space=pltpu.VMEM)
    terms = pl.pallas_call(
        functools.partial(features_kernel, device_count, slot_count, tile_count, tile_side),
        out_shape=jax.ShapeDtypeStruct((tile_count, 16 * K, pixels), jnp.bfloat16),
        in_specs=[in_smem] + [in_vmem] * device_count,
        out_specs=in_vmem,
        scratch_shapes=[pltpu.VMEM((K, tile_count, group_channels, pixels), jnp.float32)],
        name="feature_terms",
    )(tile_map, *[inputs[piece] for piece in range(device_count)])
    field = (tile_count, group_channels, pixels)
    return pl.pallas_call(
        functools.partial(
            gradient_kernel, device_count, groups, slot_count, tile_count, tile_side, scale_factor
        ),
        out_shape=(
            jax.ShapeDtypeStruct(features.shape, jnp.bfloat16),
            jax.ShapeDtypeStruct((K, group_channels, groups * group_channels), jnp.float32),
        ),
        in_specs=[in_smem] + [in_vmem] * (groups + 2),
        out_specs=(in_vmem, in_vmem),
        scratch_shapes=[
            pltpu.VMEM((tile_count, groups * group_channels, pixels), jnp.bfloat16),
            pltpu.VMEM((K, groups * group_channels, LANES), jnp.float32),
            pltpu.VMEM((tile_count, K * group_channels, pixels), jnp.float32),
            pltpu.VMEM(field, jnp.float32),
            pltpu.VMEM(field, jnp.float32),
        ],
        name="gradients",
    )(tile_map, *[by_group[other] for other in range(groups)], terms, filters)


def on_device(features, out_grad, filters, tile_map):
    slot_count, group_channels, pixels = features.shape
    device_count = lax.axis_size("tile")
    groups = lax.axis_size("sub")
    tile_side = math.isqrt(pixels)
    map_bytes = 2 * slot_count * device_count * groups * group_channels * pixels
    fits = (
        map_bytes <= GATHER_LIMIT
        and group_channels == 8
        and LANES % tile_side == 0
        and pixels % LANES == 0
        and device_count & (device_count - 1) == 0
        and groups & (groups - 1) == 0
        and groups * group_channels <= LANES
    )
    step = by_gathering if fits else by_halos
    return step(features, out_grad, filters, tile_map)


def solution(mesh):
    placed = (P(("grp", "tile"), "sub", None), P(("grp", "tile"), "sub", None), P(), P())
    return jax.shard_map(
        on_device,
        mesh=mesh,
        in_specs=placed,
        out_specs=(P(("grp", "tile"), "sub", None), P("grp", "sub", None)),
        check_vma=False,
    )
```

```python
import functools
import math

import jax
import jax.numpy as jnp
import numpy as np
from jax import lax
from jax.experimental import pallas as pl
from jax.experimental.pallas import tpu as pltpu
from jax.sharding import PartitionSpec as P


K = 5


def from_behind(value, axis, steps):
    count = lax.axis_size(axis)
    pairs = [(source, (source + steps) % count) for source in range(count)]
    return lax.ppermute(value, axis, pairs)


def tile_coords(nested_code, bit_count):
    coord_x = nested_code * 0
    coord_y = nested_code * 0
    for bit_level in range(bit_count):
        coord_x = coord_x + nested_code // 4**bit_level % 2 * 2**bit_level
        coord_y = coord_y + nested_code // (2 * 4**bit_level) % 2 * 2**bit_level
    return (coord_x, coord_y)


def nested_index(coord_x, coord_y, bit_count):
    nested_code = coord_x * 0
    for bit_level in range(bit_count):
        nested_code = nested_code + coord_x // 2**bit_level % 2 * 4**bit_level
        nested_code = nested_code + coord_y // 2**bit_level % 2 * (2 * 4**bit_level)
    return nested_code


def pick(condition, when_true, when_false):
    return when_false + (when_true - when_false) * condition


def neighbour_codes(tile_ids, per_face, side_count):
    bit_count = side_count.bit_length() - 1
    face_id = tile_ids // per_face
    coord_x, coord_y = tile_coords(tile_ids % per_face, bit_count)
    column = face_id % 4
    is_north = face_id < 4
    is_south = face_id >= 8
    last_tile = side_count - 1

    def by_cycle(north_value, equator_value, south_value):
        return pick(is_north, north_value, pick(is_south, south_value, equator_value))

    side_rules = [
        (
            coord_x > 0,
            (face_id, coord_x - 1, coord_y, 1),
            (
                by_cycle(4 + column, 8 + (column + 3) % 4, 8 + (column + 3) % 4),
                by_cycle(last_tile, last_tile, coord_y),
                by_cycle(coord_y, coord_y, 0),
                by_cycle(1, 1, 2),
            ),
        ),
        (
            coord_x < last_tile,
            (face_id, coord_x + 1, coord_y, 0),
            (
                by_cycle((column + 1) % 4, column, 4 + (column + 1) % 4),
                by_cycle(coord_y, 0, 0),
                by_cycle(last_tile, coord_y, coord_y),
                by_cycle(3, 0, 0),
            ),
        ),
        (
            coord_y > 0,
            (face_id, coord_x, coord_y - 1, 3),
            (
                by_cycle(4 + (column + 1) % 4, 8 + column, 8 + (column + 1) % 4),
                by_cycle(coord_x, coord_x, 0),
                by_cycle(last_tile, last_tile, coord_x),
                by_cycle(3, 3, 0),
            ),
        ),
        (
            coord_y < last_tile,
            (face_id, coord_x, coord_y + 1, 2),
            (
                by_cycle((column + 3) % 4, (column + 3) % 4, 4 + column),
                by_cycle(last_tile, coord_x, coord_x),
                by_cycle(coord_x, 0, 0),
                by_cycle(1, 2, 2),
            ),
        ),
    ]
    target_list = []
    edge_list = []
    for inside, within, across in side_rules:
        chosen = [
            pick(inside, near_value, far_value) for near_value, far_value in zip(within, across)
        ]
        target_list.append(chosen[0] * per_face + nested_index(chosen[1], chosen[2], bit_count))
        edge_list.append(chosen[3] + tile_ids * 0)
    return (target_list, edge_list)


def neighbour_table(tile_map, per_face, side_count):
    target_list, edge_list = neighbour_codes(tile_map, per_face, side_count)
    targets = jnp.stack(target_list, axis=1).astype(jnp.int32)
    edges = jnp.stack(edge_list, axis=1).astype(jnp.int32)
    slot_of = jnp.argsort(tile_map).astype(jnp.int32)
    return (slot_of[targets].astype(jnp.int32), edges)


def peer_offsets(slot_count, device_count, per_face, side_count):
    tile_ids = np.arange(slot_count * device_count, dtype=np.int64)
    target_list, _ = neighbour_codes(tile_ids, per_face, side_count)
    targets = np.stack(target_list, axis=1)
    offsets = (tile_ids[:, None] // slot_count - targets // slot_count) % device_count
    distinct = sorted(set((int(value) for value in offsets.ravel())) - {0})
    position = np.zeros(device_count, dtype=np.int32)
    for order, value in enumerate(distinct):
        position[value] = order + 1
    return (distinct, position)


def edge_lines(values, tile_side):
    return jnp.stack(
        [
            values[..., :tile_side],
            values[..., -tile_side:],
            values[..., ::tile_side],
            values[..., tile_side - 1 :: tile_side],
        ],
        axis=1,
    )


def stencil(values, ghosts, tile_side):
    position = jnp.arange(values.shape[-1]) % tile_side
    zero_line = jnp.zeros_like(values[..., :1])
    upper_side = jnp.concatenate([ghosts[:, 0], values[..., :-tile_side]], axis=-1)
    lower_side = jnp.concatenate([values[..., tile_side:], ghosts[:, 1]], axis=-1)
    left_side = jnp.where(
        position == 0,
        jnp.repeat(ghosts[:, 2], tile_side, axis=-1),
        jnp.concatenate([zero_line, values[..., :-1]], axis=-1),
    )
    right_side = jnp.where(
        position == tile_side - 1,
        jnp.repeat(ghosts[:, 3], tile_side, axis=-1),
        jnp.concatenate([values[..., 1:], zero_line], axis=-1),
    )
    return -0.25 * (upper_side + lower_side + left_side + right_side)


def tile_total(filter_part):
    return lax.psum(filter_part, "tile")


def by_halos(features, out_grad, filters, tile_map):
    slot_count = features.shape[0]
    group_channels = features.shape[1]
    tile_side = math.isqrt(features.shape[2])
    device_count = lax.axis_size("tile")
    total_tiles = slot_count * device_count
    side_count = math.isqrt(total_tiles // 12)
    scale_factor = 1.0 / math.sqrt(total_tiles * features.shape[2])
    highest = lax.Precision.HIGHEST
    slot_table, edge_table = neighbour_table(tile_map, total_tiles // 12, side_count)
    my_device = lax.axis_index("tile")
    first_slot = my_device * slot_count
    my_slots = lax.dynamic_slice_in_dim(slot_table, first_slot, slot_count, 0)
    my_edges = lax.dynamic_slice_in_dim(edge_table, first_slot, slot_count, 0)
    channel_start = lax.axis_index("sub") * group_channels
    weights = filters.astype(jnp.float32)
    distinct, position = peer_offsets(slot_count, device_count, total_tiles // 12, side_count)
    sender_gap = (my_device - my_slots // slot_count) % device_count
    local_rows = jnp.asarray(position)[sender_gap] * slot_count + my_slots % slot_count

    def laplace(values):
        border = edge_lines(values, tile_side).reshape(slot_count, 4, group_channels * tile_side)
        received = [border]
        for offset_value in distinct:
            received.append(from_behind(border, "tile", offset_value))
        stacked = jnp.concatenate(received, axis=0)
        stacked = stacked.reshape(stacked.shape[0], 4, group_channels, tile_side)
        ghosts = stacked[local_rows, my_edges]
        return stencil(values, ghosts, tile_side)

    whole_grad = lax.all_gather(out_grad, "sub", axis=1, tiled=True)
    cotangent = whole_grad.astype(jnp.float32)
    inputs = features.astype(jnp.float32)
    previous, current = (inputs, laplace(inputs))
    filter_terms = [
        jnp.einsum("sip,sop->io", inputs, cotangent, precision=highest),
        jnp.einsum("sip,sop->io", current, cotangent, precision=highest),
    ]
    for _ in range(2, K):
        previous, current = (current, 2.0 * laplace(current) - previous)
        filter_terms.append(jnp.einsum("sip,sop->io", current, cotangent, precision=highest))
    weight_grad = tile_total(jnp.stack(filter_terms)) * scale_factor
    row_block = lax.dynamic_slice_in_dim(weights, channel_start, group_channels, 1)

    def mixed(degree):
        return jnp.einsum("sop,io->sip", cotangent, row_block[degree], precision=highest)

    next_sum = mixed(K - 1)
    after_next = jnp.zeros_like(next_sum)
    for degree in range(K - 2, 0, -1):
        next_sum, after_next = (mixed(degree) + 2.0 * laplace(next_sum) - after_next, next_sum)
    in_grad = (mixed(0) + laplace(next_sum) - after_next).astype(jnp.bfloat16)
    return (in_grad, weight_grad)


LANES = 128
SUBLANES = 8
GATHER_LIMIT = 2 << 20
BLOCK = 256
KERNEL_BYTES = 20 << 20


def lane_iota(rows=1):
    return lax.broadcasted_iota(jnp.int32, (rows, LANES), 1)


def lane_gather(block, lane_index):
    index = jnp.broadcast_to(lane_index, block.shape)
    return jnp.take_along_axis(block, index, axis=1, mode="promise_in_bounds")


def shuffled(value, lane_index):
    parts = [
        lane_gather(value[start : start + SUBLANES], lane_index)
        for start in range(0, value.shape[0], SUBLANES)
    ]
    return jnp.concatenate(parts, axis=0)


def identity(rows, columns):
    shape = (rows, columns)
    same = lax.broadcasted_iota(jnp.int32, shape, 0) == lax.broadcasted_iota(jnp.int32, shape, 1)
    return same.astype(jnp.float32).astype(jnp.bfloat16)


def product(left, right):
    return jnp.dot(left, right, preferred_element_type=jnp.float32)


def product_of_rows(left, right):
    return lax.dot_general(
        left, right, (((1,), (1,)), ((), ())), preferred_element_type=jnp.float32
    )


def high_and_low(value):
    high = value.astype(jnp.bfloat16)
    return high, (value - high.astype(jnp.float32)).astype(jnp.bfloat16)


class Map:
    def __init__(self, map_ref, slot_count, device_count, tile_side, channels):
        self.side = tile_side
        self.pixels = tile_side * tile_side
        tile_count = slot_count * device_count
        per_face = tile_count // 12
        side_count = math.isqrt(per_face)
        targets, edges = neighbour_codes(
            np.arange(tile_count, dtype=np.int64), per_face, side_count
        )
        me = lax.axis_index("tile")
        held = [
            map_ref[(me ^ (place // slot_count)) * slot_count + place % slot_count]
            for place in range(tile_count)
        ]
        lane = lane_iota()
        channel = lane % channels
        tile = jnp.full((1, LANES), -1, jnp.int32)
        for place in range(tile_count):
            tile = jnp.where(lane // channels == place, held[place], tile)
        self.index = []
        self.polar = []
        for side in range(4):
            regular = side ^ 1
            target = jnp.full((1, LANES), -1, jnp.int32)
            polar = jnp.zeros((1, LANES), jnp.int32)
            for number in range(tile_count):
                here = tile == number
                target = jnp.where(here, int(targets[side][number]), target)
                if int(edges[side][number]) != regular:
                    polar = jnp.where(here, 1, polar)
            index = lane
            for place in range(tile_count):
                index = jnp.where(target == held[place], channels * place + channel, index)
            self.index.append(index)
            self.polar.append(polar == 1)

    def set_ghosts(self, field, left, right):
        side, pixels = self.side, self.pixels
        lines = [
            field[side : 2 * side],
            field[pixels : pixels + side],
            field[pl.ds(side, side, stride=side)],
            field[pl.ds(2 * side - 1, side, stride=side)],
        ]

        def ghost(which):
            regular = shuffled(lines[which ^ 1], self.index[which])
            turned = shuffled(lines[(2, 3, 0, 1)[which]], self.index[which])
            return jnp.where(self.polar[which], turned, regular)

        field[0:side] = ghost(0)
        field[side + pixels : 2 * side + pixels] = ghost(1)
        left[0:side] = ghost(2)
        right[SUBLANES : SUBLANES + side] = ghost(3)

    def neighbour_sum(self, field, left, right, start):
        side = self.side
        row, column = divmod(start, side)
        base = side + start
        sublane = lax.broadcasted_iota(jnp.int32, (SUBLANES, LANES), 0)

        def rows(first):
            return field[first : first + SUBLANES]

        before, after = rows(base - 1), rows(base + 1)
        if column == 0:
            before = jnp.where(sublane == 0, left[row : row + SUBLANES], before)
        if column == side - SUBLANES:
            ghost = right[row + 1 : row + 1 + SUBLANES]
            after = jnp.where(sublane == SUBLANES - 1, ghost, after)
        return (rows(base - side) + rows(base + side)) + (before + after)


def features_kernel(slot_count, device_count, tile_side, map_ref, *refs):
    piece_refs, out_ref = refs[:device_count], refs[device_count]
    fields, left, right = refs[device_count + 1 :]
    channels = piece_refs[0].shape[1]
    grid = Map(map_ref, slot_count, device_count, tile_side, channels)
    side, pixels = tile_side, tile_side * tile_side
    rows = [
        piece_refs[piece][slot].astype(jnp.float32)
        for piece in range(device_count)
        for slot in range(slot_count)
    ]
    missing = LANES - channels * len(rows)
    rows.append(jnp.zeros((missing, pixels), jnp.float32))
    inputs = jnp.concatenate(rows, axis=0).astype(jnp.bfloat16)
    one = identity(BLOCK, BLOCK)
    for start in range(0, pixels, BLOCK):
        value = product_of_rows(one, inputs[:, start : start + BLOCK])
        fields[0, side + start : side + start + BLOCK] = value
        out_ref[start : start + BLOCK, 0:LANES] = value.astype(jnp.bfloat16)
    for degree in range(1, K):
        source = fields.at[degree - 1]
        grid.set_ghosts(source, left, right)
        for start in range(0, pixels, 2 * SUBLANES):
            pair = []
            for first in (start, start + SUBLANES):
                total = grid.neighbour_sum(source, left, right, first)
                place = slice(side + first, side + first + SUBLANES)
                if degree == 1:
                    term = -0.25 * total
                else:
                    term = -0.5 * total - fields[degree - 2, place]
                fields[degree, place] = term
                pair.append(term)
            high, low = high_and_low(jnp.concatenate(pair, axis=0))
            place = slice(start, start + 2 * SUBLANES)
            first_lane = (2 * degree - 1) * LANES
            out_ref[place, first_lane : first_lane + LANES] = high
            out_ref[place, first_lane + LANES : first_lane + 2 * LANES] = low


def gradient_kernel(groups, slot_count, device_count, tile_side, scale_factor, map_ref, *refs):
    group_refs = refs[:groups]
    terms_ref, filters_ref, in_grad_ref, weight_grad_ref = refs[groups : groups + 4]
    whole, spread, mixed, fields, left, right, products = refs[groups + 4 :]
    group_channels = group_refs[0].shape[1]
    channels = groups * group_channels
    tile_count = slot_count * device_count
    side, pixels = tile_side, tile_side * tile_side
    grid = Map(map_ref, slot_count, device_count, tile_side, group_channels)
    group = lax.axis_index("sub")
    own = group * group_channels

    shape = (channels, channels)
    reorder = lax.broadcasted_iota(jnp.int32, shape, 1) == (
        lax.broadcasted_iota(jnp.int32, shape, 0) ^ own
    )
    reorder = reorder.astype(jnp.float32).astype(jnp.bfloat16)
    filter_rows = filters_ref[...].reshape(K * channels, channels)
    turned = product_of_rows(reorder, filter_rows).astype(jnp.bfloat16)
    shape = (K * channels, K * LANES)
    row = lax.broadcasted_iota(jnp.int32, shape, 0)
    lane = lax.broadcasted_iota(jnp.int32, shape, 1)
    chosen = (row // channels == lane // LANES) & (
        row % channels == own + lane % group_channels
    )
    repeated = product(turned, chosen.astype(jnp.float32).astype(jnp.bfloat16))
    lane = lax.broadcasted_iota(jnp.int32, (1, K * LANES), 1)
    for place in range(tile_count):
        mine = lane % LANES // group_channels == place
        spread[channels * place : channels * (place + 1)] = jnp.where(
            mine, repeated, 0.0
        ).astype(jnp.bfloat16)

    for place in range(tile_count):
        rows = [group_refs[other][place].astype(jnp.float32) for other in range(groups)]
        whole[channels * place : channels * (place + 1)] = jnp.concatenate(rows, axis=0).astype(
            jnp.bfloat16
        )
    one = identity(BLOCK, BLOCK)
    for start in range(0, pixels, BLOCK):
        turned = product_of_rows(one, whole[:, start : start + BLOCK]).astype(jnp.bfloat16)
        value = product(turned, spread[...])
        for degree in range(K - 1):
            lanes = slice(LANES * degree, LANES * (degree + 1))
            mixed[degree, start : start + BLOCK] = value[:, lanes]
        fields[0, side + start : side + start + BLOCK] = value[:, LANES * (K - 1) :]

    products[...] = product(whole[...], terms_ref[...])
    lane = lane_iota()
    sums = []
    for degree in range(K):
        total = jnp.zeros((channels, LANES), jnp.float32)
        for place in range(tile_count):
            rows = slice(channels * place, channels * (place + 1))
            if degree == 0:
                part = products[rows, 0:LANES]
            else:
                first_lane = (2 * degree - 1) * LANES
                part = (
                    products[rows, first_lane : first_lane + LANES]
                    + products[rows, first_lane + LANES : first_lane + 2 * LANES]
                )
            total = total + jnp.where(lane // group_channels == place, part, 0.0)
        distance = group_channels
        while distance < LANES:
            total = total + pltpu.roll(total, distance, 1)
            distance *= 2
        sums.append(total)
    packed = sums[0]
    for degree in range(1, K):
        packed = jnp.where(lane // group_channels == degree, sums[degree], packed)
    packed = jnp.concatenate(
        [packed * scale_factor, jnp.zeros((LANES - channels, LANES), jnp.float32)], axis=0
    )
    turned = packed.T
    order = jnp.where(lane < channels, lane ^ own, lane)
    for degree in range(K):
        rows = turned[group_channels * degree : group_channels * (degree + 1)]
        weight_grad_ref[degree] = lane_gather(rows, order)[:, :channels]

    current, other = 0, 1
    for degree in range(K - 2, -1, -1):
        source, result = fields.at[current], fields.at[other]
        grid.set_ghosts(source, left, right)
        factor = -0.5 if degree > 0 else -0.25
        for start in range(0, pixels, SUBLANES):
            total = grid.neighbour_sum(source, left, right, start)
            value = mixed[degree, start : start + SUBLANES] + factor * total
            place = slice(side + start, side + start + SUBLANES)
            if degree < K - 2:
                value = value - result[place]
            result[place] = value
        current, other = other, current
    rows = slot_count * group_channels
    rows += -rows % 16
    pick_both = jnp.concatenate([identity(rows, LANES), identity(rows, LANES)], axis=1)
    for start in range(0, pixels, BLOCK):
        place = slice(side + start, side + start + BLOCK)
        both = jnp.concatenate(high_and_low(fields[current, place]), axis=1)
        value = product_of_rows(pick_both, both)
        for slot in range(slot_count):
            first_row = group_channels * slot
            in_grad_ref[slot, :, start : start + BLOCK] = value[
                first_row : first_row + group_channels
            ].astype(jnp.bfloat16)


def by_gathering(features, out_grad, filters, tile_map):
    slot_count, group_channels, pixels = features.shape
    tile_side = math.isqrt(pixels)
    device_count = lax.axis_size("tile")
    groups = lax.axis_size("sub")
    tile_count = slot_count * device_count
    channels = groups * group_channels
    scale_factor = 1.0 / math.sqrt(tile_count * pixels)

    def exchanged(value, axis, distance):
        count = lax.axis_size(axis)
        return lax.ppermute(
            value, axis, [(index, index ^ distance) for index in range(count)]
        )

    order = range(device_count - 1, 0, -1)
    cotangents = {0: out_grad}
    for distance in order:
        cotangents[distance] = exchanged(out_grad, "tile", distance)
    inputs = {0: features}
    for distance in order:
        inputs[distance] = exchanged(features, "tile", distance)
    stacked = jnp.concatenate([cotangents[piece] for piece in range(device_count)], axis=0)
    by_group = {0: stacked}
    distance = groups // 2
    while distance:
        for known in list(by_group):
            by_group[known + distance] = exchanged(by_group[known], "sub", distance)
        distance //= 2

    in_smem = pl.BlockSpec(memory_space=pltpu.SMEM)
    in_vmem = pl.BlockSpec(memory_space=pltpu.VMEM)
    field = (pixels + 2 * tile_side, LANES)
    beside = pltpu.VMEM((tile_side + SUBLANES, LANES), jnp.float32)
    parts = 2 * K - 1
    terms = pl.pallas_call(
        functools.partial(features_kernel, slot_count, device_count, tile_side),
        out_shape=jax.ShapeDtypeStruct((pixels, parts * LANES), jnp.bfloat16),
        in_specs=[in_smem] + [in_vmem] * device_count,
        out_specs=in_vmem,
        scratch_shapes=[pltpu.VMEM((K,) + field, jnp.float32), beside, beside],
        compiler_params=pltpu.CompilerParams(vmem_limit_bytes=KERNEL_BYTES),
        cost_estimate=pl.CostEstimate(
            flops=4 * 10**9, bytes_accessed=10**6, transcendentals=0
        ),
        name="feature_terms",
    )(tile_map, *[inputs[piece] for piece in range(device_count)])
    return pl.pallas_call(
        functools.partial(
            gradient_kernel, groups, slot_count, device_count, tile_side, scale_factor
        ),
        out_shape=(
            jax.ShapeDtypeStruct(features.shape, jnp.bfloat16),
            jax.ShapeDtypeStruct((K, group_channels, channels), jnp.float32),
        ),
        in_specs=[in_smem] + [in_vmem] * (groups + 2),
        out_specs=(in_vmem, in_vmem),
        scratch_shapes=[
            pltpu.VMEM((tile_count * channels, pixels), jnp.bfloat16),
            pltpu.VMEM((tile_count * channels, K * LANES), jnp.bfloat16),
            pltpu.VMEM((K - 1, pixels, LANES), jnp.float32),
            pltpu.VMEM((2,) + field, jnp.float32),
            beside,
            beside,
            pltpu.VMEM((tile_count * channels, parts * LANES), jnp.float32),
        ],
        compiler_params=pltpu.CompilerParams(vmem_limit_bytes=KERNEL_BYTES),
        name="gradients",
    )(tile_map, *[by_group[other] for other in range(groups)], terms, filters)


def on_device(features, out_grad, filters, tile_map):
    slot_count, group_channels, pixels = features.shape
    device_count = lax.axis_size("tile")
    groups = lax.axis_size("sub")
    tile_side = math.isqrt(pixels)
    map_bytes = 2 * slot_count * device_count * groups * group_channels * pixels
    fits = (
        map_bytes <= GATHER_LIMIT
        and group_channels == SUBLANES
        and slot_count * device_count * group_channels < LANES
        and K * group_channels <= LANES
        and tile_side % 16 == 0
        and pixels % BLOCK == 0
        and device_count & (device_count - 1) == 0
        and groups & (groups - 1) == 0
        and groups * group_channels <= LANES
    )
    step = by_gathering if fits else by_halos
    return step(features, out_grad, filters, tile_map)


def solution(mesh):
    placed = (P(("grp", "tile"), "sub", None), P(("grp", "tile"), "sub", None), P(), P())
    return jax.shard_map(
        on_device,
        mesh=mesh,
        in_specs=placed,
        out_specs=(P(("grp", "tile"), "sub", None), P("grp", "sub", None)),
        check_vma=False,
    )
```

```python
import functools
import math

import jax
import jax.numpy as jnp
import numpy as np
from jax import lax
from jax.experimental import pallas as pl
from jax.experimental.pallas import tpu as pltpu
from jax.sharding import PartitionSpec as P


K = 5


def from_behind(value, axis, steps):
    count = lax.axis_size(axis)
    pairs = [(source, (source + steps) % count) for source in range(count)]
    return lax.ppermute(value, axis, pairs)


def tile_coords(nested_code, bit_count):
    coord_x = nested_code * 0
    coord_y = nested_code * 0
    for bit_level in range(bit_count):
        coord_x = coord_x + nested_code // 4**bit_level % 2 * 2**bit_level
        coord_y = coord_y + nested_code // (2 * 4**bit_level) % 2 * 2**bit_level
    return (coord_x, coord_y)


def nested_index(coord_x, coord_y, bit_count):
    nested_code = coord_x * 0
    for bit_level in range(bit_count):
        nested_code = nested_code + coord_x // 2**bit_level % 2 * 4**bit_level
        nested_code = nested_code + coord_y // 2**bit_level % 2 * (2 * 4**bit_level)
    return nested_code


def pick(condition, when_true, when_false):
    return when_false + (when_true - when_false) * condition


def neighbour_codes(tile_ids, per_face, side_count):
    bit_count = side_count.bit_length() - 1
    face_id = tile_ids // per_face
    coord_x, coord_y = tile_coords(tile_ids % per_face, bit_count)
    column = face_id % 4
    is_north = face_id < 4
    is_south = face_id >= 8
    last_tile = side_count - 1

    def by_cycle(north_value, equator_value, south_value):
        return pick(is_north, north_value, pick(is_south, south_value, equator_value))

    side_rules = [
        (
            coord_x > 0,
            (face_id, coord_x - 1, coord_y, 1),
            (
                by_cycle(4 + column, 8 + (column + 3) % 4, 8 + (column + 3) % 4),
                by_cycle(last_tile, last_tile, coord_y),
                by_cycle(coord_y, coord_y, 0),
                by_cycle(1, 1, 2),
            ),
        ),
        (
            coord_x < last_tile,
            (face_id, coord_x + 1, coord_y, 0),
            (
                by_cycle((column + 1) % 4, column, 4 + (column + 1) % 4),
                by_cycle(coord_y, 0, 0),
                by_cycle(last_tile, coord_y, coord_y),
                by_cycle(3, 0, 0),
            ),
        ),
        (
            coord_y > 0,
            (face_id, coord_x, coord_y - 1, 3),
            (
                by_cycle(4 + (column + 1) % 4, 8 + column, 8 + (column + 1) % 4),
                by_cycle(coord_x, coord_x, 0),
                by_cycle(last_tile, last_tile, coord_x),
                by_cycle(3, 3, 0),
            ),
        ),
        (
            coord_y < last_tile,
            (face_id, coord_x, coord_y + 1, 2),
            (
                by_cycle((column + 3) % 4, (column + 3) % 4, 4 + column),
                by_cycle(last_tile, coord_x, coord_x),
                by_cycle(coord_x, 0, 0),
                by_cycle(1, 2, 2),
            ),
        ),
    ]
    target_list = []
    edge_list = []
    for inside, within, across in side_rules:
        chosen = [
            pick(inside, near_value, far_value) for near_value, far_value in zip(within, across)
        ]
        target_list.append(chosen[0] * per_face + nested_index(chosen[1], chosen[2], bit_count))
        edge_list.append(chosen[3] + tile_ids * 0)
    return (target_list, edge_list)


def neighbour_table(tile_map, per_face, side_count):
    target_list, edge_list = neighbour_codes(tile_map, per_face, side_count)
    targets = jnp.stack(target_list, axis=1).astype(jnp.int32)
    edges = jnp.stack(edge_list, axis=1).astype(jnp.int32)
    slot_of = jnp.argsort(tile_map).astype(jnp.int32)
    return (slot_of[targets].astype(jnp.int32), edges)


def peer_offsets(slot_count, device_count, per_face, side_count):
    tile_ids = np.arange(slot_count * device_count, dtype=np.int64)
    target_list, _ = neighbour_codes(tile_ids, per_face, side_count)
    targets = np.stack(target_list, axis=1)
    offsets = (tile_ids[:, None] // slot_count - targets // slot_count) % device_count
    distinct = sorted(set((int(value) for value in offsets.ravel())) - {0})
    position = np.zeros(device_count, dtype=np.int32)
    for order, value in enumerate(distinct):
        position[value] = order + 1
    return (distinct, position)


def edge_lines(values, tile_side):
    return jnp.stack(
        [
            values[..., :tile_side],
            values[..., -tile_side:],
            values[..., ::tile_side],
            values[..., tile_side - 1 :: tile_side],
        ],
        axis=1,
    )


def stencil(values, ghosts, tile_side):
    position = jnp.arange(values.shape[-1]) % tile_side
    zero_line = jnp.zeros_like(values[..., :1])
    upper_side = jnp.concatenate([ghosts[:, 0], values[..., :-tile_side]], axis=-1)
    lower_side = jnp.concatenate([values[..., tile_side:], ghosts[:, 1]], axis=-1)
    left_side = jnp.where(
        position == 0,
        jnp.repeat(ghosts[:, 2], tile_side, axis=-1),
        jnp.concatenate([zero_line, values[..., :-1]], axis=-1),
    )
    right_side = jnp.where(
        position == tile_side - 1,
        jnp.repeat(ghosts[:, 3], tile_side, axis=-1),
        jnp.concatenate([values[..., 1:], zero_line], axis=-1),
    )
    return -0.25 * (upper_side + lower_side + left_side + right_side)


def tile_total(filter_part):
    return lax.psum(filter_part, "tile")


def by_halos(features, out_grad, filters, tile_map):
    slot_count = features.shape[0]
    group_channels = features.shape[1]
    tile_side = math.isqrt(features.shape[2])
    device_count = lax.axis_size("tile")
    total_tiles = slot_count * device_count
    side_count = math.isqrt(total_tiles // 12)
    scale_factor = 1.0 / math.sqrt(total_tiles * features.shape[2])
    highest = lax.Precision.HIGHEST
    slot_table, edge_table = neighbour_table(tile_map, total_tiles // 12, side_count)
    my_device = lax.axis_index("tile")
    first_slot = my_device * slot_count
    my_slots = lax.dynamic_slice_in_dim(slot_table, first_slot, slot_count, 0)
    my_edges = lax.dynamic_slice_in_dim(edge_table, first_slot, slot_count, 0)
    channel_start = lax.axis_index("sub") * group_channels
    weights = filters.astype(jnp.float32)
    distinct, position = peer_offsets(slot_count, device_count, total_tiles // 12, side_count)
    sender_gap = (my_device - my_slots // slot_count) % device_count
    local_rows = jnp.asarray(position)[sender_gap] * slot_count + my_slots % slot_count

    def laplace(values):
        border = edge_lines(values, tile_side).reshape(slot_count, 4, group_channels * tile_side)
        received = [border]
        for offset_value in distinct:
            received.append(from_behind(border, "tile", offset_value))
        stacked = jnp.concatenate(received, axis=0)
        stacked = stacked.reshape(stacked.shape[0], 4, group_channels, tile_side)
        ghosts = stacked[local_rows, my_edges]
        return stencil(values, ghosts, tile_side)

    whole_grad = lax.all_gather(out_grad, "sub", axis=1, tiled=True)
    cotangent = whole_grad.astype(jnp.float32)
    inputs = features.astype(jnp.float32)
    previous, current = (inputs, laplace(inputs))
    filter_terms = [
        jnp.einsum("sip,sop->io", inputs, cotangent, precision=highest),
        jnp.einsum("sip,sop->io", current, cotangent, precision=highest),
    ]
    for _ in range(2, K):
        previous, current = (current, 2.0 * laplace(current) - previous)
        filter_terms.append(jnp.einsum("sip,sop->io", current, cotangent, precision=highest))
    weight_grad = tile_total(jnp.stack(filter_terms)) * scale_factor
    row_block = lax.dynamic_slice_in_dim(weights, channel_start, group_channels, 1)

    def mixed(degree):
        return jnp.einsum("sop,io->sip", cotangent, row_block[degree], precision=highest)

    next_sum = mixed(K - 1)
    after_next = jnp.zeros_like(next_sum)
    for degree in range(K - 2, 0, -1):
        next_sum, after_next = (mixed(degree) + 2.0 * laplace(next_sum) - after_next, next_sum)
    in_grad = (mixed(0) + laplace(next_sum) - after_next).astype(jnp.bfloat16)
    return (in_grad, weight_grad)


LANES = 128
SUBLANES = 8
GATHER_LIMIT = 2 << 20
BLOCK = 256
KERNEL_BYTES = 20 << 20


def lane_iota(rows=1):
    return lax.broadcasted_iota(jnp.int32, (rows, LANES), 1)


def lane_gather(block, lane_index):
    index = jnp.broadcast_to(lane_index, block.shape)
    return jnp.take_along_axis(block, index, axis=1, mode="promise_in_bounds")


def shuffled(value, lane_index):
    parts = [
        lane_gather(value[start : start + SUBLANES], lane_index)
        for start in range(0, value.shape[0], SUBLANES)
    ]
    return jnp.concatenate(parts, axis=0)


def identity(rows, columns):
    shape = (rows, columns)
    same = lax.broadcasted_iota(jnp.int32, shape, 0) == lax.broadcasted_iota(jnp.int32, shape, 1)
    return same.astype(jnp.float32).astype(jnp.bfloat16)


def product(left, right):
    return jnp.dot(left, right, preferred_element_type=jnp.float32)


def product_of_rows(left, right):
    return lax.dot_general(
        left, right, (((1,), (1,)), ((), ())), preferred_element_type=jnp.float32
    )


def high_and_low(value):
    high = value.astype(jnp.bfloat16)
    return high, (value - high.astype(jnp.float32)).astype(jnp.bfloat16)


def ghost_tables(map_ref, slot_count, device_count, channels):
    tile_count = slot_count * device_count
    per_face = tile_count // 12
    targets, edges = neighbour_codes(
        np.arange(tile_count, dtype=np.int64), per_face, math.isqrt(per_face)
    )
    me = lax.axis_index("tile")
    held = [
        map_ref[(me ^ (place // slot_count)) * slot_count + place % slot_count]
        for place in range(tile_count)
    ]
    shape = (SUBLANES, LANES)
    lane = lax.broadcasted_iota(jnp.int32, shape, 1)
    side = lax.broadcasted_iota(jnp.int32, shape, 0)
    tile = jnp.full(shape, -1, jnp.int32)
    for place in range(tile_count):
        tile = jnp.where(lane // channels == place, held[place], tile)
    target = jnp.full(shape, -1, jnp.int32)
    turned = jnp.zeros(shape, jnp.int32)
    for number in range(tile_count):
        wanted = jnp.zeros(shape, jnp.int32)
        for which in range(4):
            wanted = jnp.where(side == which, int(targets[which][number]), wanted)
            if int(edges[which][number]) != which ^ 1:
                turned = jnp.where((side == which + 4) & (tile == number), 1, turned)
        target = jnp.where(tile == number, wanted, target)
    index = lane
    for place in range(tile_count):
        index = jnp.where(target == held[place], channels * place + lane % channels, index)
    return jnp.where(side < 4, index, turned)


class Map:
    def __init__(self, tables_ref, tile_side):
        self.side = tile_side
        self.pixels = tile_side * tile_side
        self.index = [tables_ref[which : which + 1] for which in range(4)]
        self.turned = [tables_ref[which + 4 : which + 5] == 1 for which in range(4)]

    def set_ghosts(self, field, left, right):
        side, pixels = self.side, self.pixels
        lines = [
            field[side : 2 * side],
            field[pixels : pixels + side],
            field[pl.ds(side, side, stride=side)],
            field[pl.ds(2 * side - 1, side, stride=side)],
        ]

        def ghost(which):
            regular = shuffled(lines[which ^ 1], self.index[which])
            turned = shuffled(lines[(2, 3, 0, 1)[which]], self.index[which])
            return jnp.where(self.turned[which], turned, regular)

        field[0:side] = ghost(0)
        field[side + pixels : 2 * side + pixels] = ghost(1)
        left[0:side] = ghost(2)
        right[SUBLANES : SUBLANES + side] = ghost(3)

    def neighbour_sum(self, field, left, right, start):
        side = self.side
        row, column = divmod(start, side)
        base = side + start
        sublane = lax.broadcasted_iota(jnp.int32, (SUBLANES, LANES), 0)

        def rows(first):
            return field[first : first + SUBLANES]

        before, after = rows(base - 1), rows(base + 1)
        if column == 0:
            before = jnp.where(sublane == 0, left[row : row + SUBLANES], before)
        if column == side - SUBLANES:
            ghost = right[row + 1 : row + 1 + SUBLANES]
            after = jnp.where(sublane == SUBLANES - 1, ghost, after)
        return (rows(base - side) + rows(base + side)) + (before + after)


def stack_rows(group_refs, whole, first):
    for tile in range(group_refs[0].shape[0]):
        rows = [ref[tile].astype(jnp.float32) for ref in group_refs]
        rows = jnp.concatenate(rows, axis=0).astype(jnp.bfloat16)
        whole[first : first + rows.shape[0]] = rows
        first += rows.shape[0]


def turn_rows(whole, turned):
    one = identity(BLOCK, BLOCK)
    for start in range(0, whole.shape[1], BLOCK):
        turned[start : start + BLOCK] = product_of_rows(
            one, whole[:, start : start + BLOCK]
        ).astype(jnp.bfloat16)


def mix_rows(turned, spread, store):
    for first in range(0, K, 2):
        count = min(2, K - first)
        value = product(turned[...], spread[:, LANES * first : LANES * (first + count)])
        for number in range(count):
            store(K - 1 - first - number, value[:, LANES * number : LANES * (number + 1)])


def near_kernel(slot_count, device_count, near, filters_ref, *refs):
    rest_refs, refs = refs[:near], refs[near:]
    far_spread, whole, mixed, near_spread, turned = refs
    group_channels = rest_refs[0].shape[1]
    stack_rows(rest_refs, whole, 0)
    turn_rows(whole, turned)
    channels = filters_ref.shape[1]
    half = channels // 2
    own = lax.axis_index("sub") * group_channels
    shape = (channels, channels)
    reorder = lax.broadcasted_iota(jnp.int32, shape, 1) == (
        lax.broadcasted_iota(jnp.int32, shape, 0) ^ own
    )
    reorder = reorder.astype(jnp.float32).astype(jnp.bfloat16)
    filter_rows = filters_ref[...].reshape(K * channels, channels)
    filter_columns = product_of_rows(reorder, filter_rows).astype(jnp.bfloat16)
    shape = (channels, LANES)
    row = lax.broadcasted_iota(jnp.int32, shape, 0)
    lane = lax.broadcasted_iota(jnp.int32, shape, 1)
    chosen = (row == own + lane % group_channels).astype(jnp.float32).astype(jnp.bfloat16)
    for order, degree in enumerate(range(K - 1, -1, -1)):
        repeated = product(filter_columns[:, channels * degree : channels * (degree + 1)], chosen)
        for place in range(slot_count * device_count):
            mine = jnp.where(lane // group_channels == place, repeated, 0.0).astype(jnp.bfloat16)
            lanes = slice(LANES * order, LANES * (order + 1))
            if place < slot_count:
                far_spread[channels * place : channels * (place + 1), lanes] = mine
            else:
                first = half * (place - slot_count)
                near_spread[first : first + half, lanes] = mine[:half]
                first += channels * slot_count
                far_spread[first : first + half, lanes] = mine[half:]

    def store(degree, value):
        mixed[degree] = value

    mix_rows(turned, near_spread, store)


def features_kernel(slot_count, device_count, tile_side, after_ref, map_ref, *refs):
    piece_refs, refs = refs[:device_count], refs[device_count:]
    out_ref, tables_ref, fields, parts, left, right = refs
    channels = piece_refs[0].shape[1]
    tables_ref[...] = ghost_tables(map_ref, slot_count, device_count, channels)
    grid = Map(tables_ref, tile_side)
    side, pixels = tile_side, tile_side * tile_side
    rows = [
        piece_refs[piece][slot].astype(jnp.float32)
        for piece in range(device_count)
        for slot in range(slot_count)
    ]
    nothing = jnp.zeros((channels, pixels), jnp.float32)
    for place, values in enumerate(rows):
        out_ref[place, 0 : 2 * channels] = jnp.concatenate([values, nothing], axis=0).astype(
            jnp.bfloat16
        )
    tile_count = len(rows)
    rows += [nothing] * (LANES // channels - tile_count)
    inputs = jnp.concatenate(rows, axis=0).astype(jnp.bfloat16)
    one = identity(BLOCK, BLOCK)
    for start in range(0, pixels, BLOCK):
        fields[0, side + start : side + start + BLOCK] = product_of_rows(
            one, inputs[:, start : start + BLOCK]
        )
    shape = (2 * channels * tile_count, 2 * LANES)
    row = lax.broadcasted_iota(jnp.int32, shape, 0)
    lane = lax.broadcasted_iota(jnp.int32, shape, 1)
    half = row // channels % 2
    source_lane = LANES * half + channels * (row // (2 * channels)) + row % channels
    pick = (lane == source_lane).astype(jnp.float32).astype(jnp.bfloat16)
    for degree in range(1, K):
        source = fields.at[degree - 1]
        grid.set_ghosts(source, left, right)
        for start in range(0, pixels, 2 * SUBLANES):
            pair = []
            for first in (start, start + SUBLANES):
                total = grid.neighbour_sum(source, left, right, first)
                place = slice(side + first, side + first + SUBLANES)
                if degree == 1:
                    term = -0.25 * total
                else:
                    term = -0.5 * total - fields[degree - 2, place]
                fields[degree, place] = term
                pair.append(term)
            high, low = high_and_low(jnp.concatenate(pair, axis=0))
            parts[degree - 1, start : start + 2 * SUBLANES, 0:LANES] = high
            parts[degree - 1, start : start + 2 * SUBLANES, LANES : 2 * LANES] = low
        for start in range(0, pixels, BLOCK):
            turned = product_of_rows(pick, parts[degree - 1, start : start + BLOCK]).astype(
                jnp.bfloat16
            )
            for place in range(tile_count):
                out_ref[
                    place,
                    2 * channels * degree : 2 * channels * (degree + 1),
                    start : start + BLOCK,
                ] = turned[2 * channels * place : 2 * channels * (place + 1)]


def gradient_kernel(
    far, slot_count, device_count, tile_side, scale_factor, tables_ref, spread_ref, *refs
):
    own_refs, rest_refs, refs = refs[: 2 * far], refs[2 * far : 3 * far], refs[3 * far :]
    terms_ref, near_whole, near_mixed, in_grad_ref, weight_grad_ref = refs[:5]
    whole, turned, mixed, fields, left, right = refs[5:]
    group_channels = own_refs[0].shape[1]
    half = group_channels * far
    channels = 2 * half
    tile_count = slot_count * device_count
    side, pixels = tile_side, tile_side * tile_side
    grid = Map(tables_ref, tile_side)
    own = lax.axis_index("sub") * group_channels

    stack_rows(own_refs, whole, 0)
    stack_rows(rest_refs, whole, channels * slot_count)
    turn_rows(whole, turned)

    def store(degree, value):
        value = value + near_mixed[degree]
        if degree == K - 1:
            fields[0, side : side + pixels] = value
        else:
            mixed[degree] = value

    mix_rows(turned, spread_ref, store)

    total = jnp.zeros((2 * group_channels * K, channels), jnp.float32)
    for place in range(tile_count):
        if place < slot_count:
            both = whole[channels * place : channels * (place + 1)]
        else:
            first = half * (place - slot_count)
            near = near_whole[first : first + half]
            first += channels * slot_count
            both = jnp.concatenate([near, whole[first : first + half]], axis=0)
        total = total + product_of_rows(terms_ref[place], both)
    total = jnp.concatenate(
        [total * scale_factor, jnp.zeros((total.shape[0], LANES - channels), jnp.float32)], axis=1
    )
    lane = lane_iota()
    order = jnp.where(lane < channels, lane ^ own, lane)
    for degree in range(K):
        first = 2 * group_channels * degree
        both = total[first : first + group_channels]
        both = both + total[first + group_channels : first + 2 * group_channels]
        weight_grad_ref[degree] = lane_gather(both, order)[:, :channels]

    current, other = 0, 1
    for degree in range(K - 2, -1, -1):
        source, result = fields.at[current], fields.at[other]
        grid.set_ghosts(source, left, right)
        factor = -0.5 if degree > 0 else -0.25
        for start in range(0, pixels, SUBLANES):
            neighbours = grid.neighbour_sum(source, left, right, start)
            value = mixed[degree, start : start + SUBLANES] + factor * neighbours
            place = slice(side + start, side + start + SUBLANES)
            if degree < K - 2:
                value = value - result[place]
            result[place] = value
        current, other = other, current
    for start in range(0, pixels, LANES):
        value = fields[current, side + start : side + start + LANES].T
        for slot in range(slot_count):
            rows = slice(group_channels * slot, group_channels * (slot + 1))
            in_grad_ref[slot, :, start : start + LANES] = value[rows].astype(jnp.bfloat16)


def by_gathering(features, out_grad, filters, tile_map):
    slot_count, group_channels, pixels = features.shape
    tile_side = math.isqrt(pixels)
    device_count = lax.axis_size("tile")
    groups = lax.axis_size("sub")
    tile_count = slot_count * device_count
    channels = groups * group_channels
    scale_factor = 1.0 / math.sqrt(tile_count * pixels)

    def exchanged(value, axis, distance):
        count = lax.axis_size(axis)
        return lax.ppermute(
            value, axis, [(index, index ^ distance) for index in range(count)]
        )

    in_smem = pl.BlockSpec(memory_space=pltpu.SMEM)
    in_vmem = pl.BlockSpec(memory_space=pltpu.VMEM)
    half = channels // 2
    params = pltpu.CompilerParams(vmem_limit_bytes=KERNEL_BYTES)

    order = range(device_count - 1, 0, -1)
    cotangents = {}
    for distance in order:
        cotangents[distance] = exchanged(out_grad, "tile", distance)
    inputs = {0: features}
    for distance in order:
        inputs[distance] = exchanged(features, "tile", distance)
    stacked = jnp.concatenate([cotangents[piece] for piece in range(1, device_count)], axis=0)

    def over_groups(value):
        known = {0: value}
        distance = groups // 2
        while distance:
            for other in list(known):
                known[other + distance] = exchanged(known[other], "sub", distance)
            distance //= 2
        return [known[other] for other in range(groups)]

    own = over_groups(out_grad)
    filters = exchanged(filters, "sub", 1)
    rest = over_groups(stacked)

    field = (pixels + 2 * tile_side, LANES)
    beside = pltpu.VMEM((tile_side + SUBLANES, LANES), jnp.float32)
    near_rows = (tile_count - slot_count) * half
    far_rows = near_rows + slot_count * channels
    near_groups = rest[: groups // 2]
    far_groups = own + rest[groups // 2 :]

    def cost(flops):
        return pl.CostEstimate(flops=flops, bytes_accessed=10**6, transcendentals=0)

    far_spread, near_whole, near_mixed = pl.pallas_call(
        functools.partial(near_kernel, slot_count, device_count, groups // 2),
        out_shape=(
            jax.ShapeDtypeStruct((far_rows, K * LANES), jnp.bfloat16),
            jax.ShapeDtypeStruct((near_rows, pixels), jnp.bfloat16),
            jax.ShapeDtypeStruct((K, pixels, LANES), jnp.float32),
        ),
        in_specs=[in_vmem] * (1 + groups // 2),
        out_specs=(in_vmem,) * 3,
        scratch_shapes=[
            pltpu.VMEM((near_rows, K * LANES), jnp.bfloat16),
            pltpu.VMEM((pixels, near_rows), jnp.bfloat16),
        ],
        compiler_params=params,
        cost_estimate=cost(2 * 10**9),
        name="near_half",
    )(filters, *near_groups)
    terms, tables = pl.pallas_call(
        functools.partial(features_kernel, slot_count, device_count, tile_side),
        out_shape=(
            jax.ShapeDtypeStruct((tile_count, 2 * group_channels * K, pixels), jnp.bfloat16),
            jax.ShapeDtypeStruct((SUBLANES, LANES), jnp.int32),
        ),
        in_specs=[pl.BlockSpec(memory_space=pl.ANY), in_smem] + [in_vmem] * device_count,
        out_specs=(in_vmem, in_vmem),
        scratch_shapes=[
            pltpu.VMEM((K,) + field, jnp.float32),
            pltpu.VMEM((K - 1, pixels, 2 * LANES), jnp.bfloat16),
            beside,
            beside,
        ],
        compiler_params=params,
        cost_estimate=cost(8 * 10**9),
        name="feature_terms",
    )(far_spread, tile_map, *[inputs[piece] for piece in range(device_count)])
    return pl.pallas_call(
        functools.partial(
            gradient_kernel, groups // 2, slot_count, device_count, tile_side, scale_factor
        ),
        out_shape=(
            jax.ShapeDtypeStruct(features.shape, jnp.bfloat16),
            jax.ShapeDtypeStruct((K, group_channels, channels), jnp.float32),
        ),
        in_specs=[in_vmem] * (5 + groups + groups // 2),
        out_specs=(in_vmem, in_vmem),
        scratch_shapes=[
            pltpu.VMEM((far_rows, pixels), jnp.bfloat16),
            pltpu.VMEM((pixels, far_rows), jnp.bfloat16),
            pltpu.VMEM((K - 1, pixels, LANES), jnp.float32),
            pltpu.VMEM((2,) + field, jnp.float32),
            beside,
            beside,
        ],
        compiler_params=pltpu.CompilerParams(vmem_limit_bytes=KERNEL_BYTES),
        name="gradients",
    )(tables, far_spread, *far_groups, terms, near_whole, near_mixed)


def on_device(features, out_grad, filters, tile_map):
    slot_count, group_channels, pixels = features.shape
    device_count = lax.axis_size("tile")
    groups = lax.axis_size("sub")
    tile_side = math.isqrt(pixels)
    map_bytes = 2 * slot_count * device_count * groups * group_channels * pixels
    fits = (
        map_bytes <= GATHER_LIMIT
        and group_channels == SUBLANES
        and slot_count * device_count * group_channels < LANES
        and K * group_channels <= LANES
        and tile_side % 16 == 0
        and pixels % BLOCK == 0
        and device_count & (device_count - 1) == 0
        and groups & (groups - 1) == 0
        and groups > 1
        and groups // 2 * group_channels % 16 == 0
        and groups * group_channels <= LANES
    )
    step = by_gathering if fits else by_halos
    return step(features, out_grad, filters, tile_map)


def solution(mesh):
    placed = (P(("grp", "tile"), "sub", None), P(("grp", "tile"), "sub", None), P(), P())
    return jax.shard_map(
        on_device,
        mesh=mesh,
        in_specs=placed,
        out_specs=(P(("grp", "tile"), "sub", None), P("grp", "sub", None)),
        check_vma=False,
    )
```
